32 devices in a mesh: batch: 8 (over z, y), dim: 4 (over x, core).
Axes of the slice: x: 2, y: 2, z: 4, core: 2. Of those that a mesh axis runs over, the one named last changes fastest.
Arguments:
- x_start: float32 [1024], P('dim'), may hold values from 0.5 to 2
- y_start: float32 [], replicated, may hold values from -1 to 1
- z_start: float32 [1024], P('dim'), may hold values from -3 to 3
- increments: float32 [5, 2048, 1024], P(None, 'batch', 'dim'), may hold values from -2.7 to 2.7
- default_step: int32 [2048], P('batch'), may hold values from 0 to 6
- term_weight: float32 [1024], P('dim'), may hold values from -6 to 6
- w_first: bfloat16 [4, 1024, 1024], P(None, None, 'dim'), may hold values from -0.1875 to 0.1875
- w_second: bfloat16 [4, 1024, 1024], P(None, 'dim'), may hold values from -0.1875 to 0.1875
- w_third: bfloat16 [4, 1024, 1024], P(None, None, 'dim'), may hold values from -0.1875 to 0.1875
Outputs:
- loss: float32 [], replicated
- grad_y: float32 [], replicated
- grad_z: float32 [1024], P('dim')
- grad_first: bfloat16 [4, 1024, 1024], P(None, None, 'dim')
- grad_second: bfloat16 [4, 1024, 1024], P(None, 'dim')
- grad_third: bfloat16 [4, 1024, 1024], P(None, None, 'dim')
The draws below stay inside these ranges and needn't reach their ends.
Inputs may be any that keep to these rules, and one draw needn't show every extreme that they name: `default_step`: the time step at which a path defaults; 5 or more means no default within the window.
All inputs are finite; a program needn't handle non-finite values.
Results may differ from the reference program's by a relative error of at most 0.0085.
Values may be sent and summed in bfloat16 or wider, within the bound.
A program may use at most 64 MiB of HBM per device.

```python
import math
import jax
import jax.numpy as jnp
from jax import lax

D = 1024
H = 1024
NETS = 4
STEPS = 5
PATHS = 2048


def with_ends(entries, rng, least, top_value):
    longest = entries.shape.index(max(entries.shape))
    spots = []
    for shift in (0, 1):
        where = [jax.random.randint(jax.random.fold_in(rng, axis), (), 0, length) for axis, length in enumerate(entries.shape)]
        where[longest] = (where[longest] + shift) % entries.shape[longest]
        spots.append(tuple(where))
    return entries.at[spots[0]].set(least).at[spots[1]].set(top_value)


def shard_levels(key, extent, split, smallest, largest):
    gain = 1.0
    for dim, blocks in split:
        heights = jax.random.uniform(jax.random.fold_in(jax.random.fold_in(key, 6), dim), (blocks,), jnp.float32, smallest / len(split), largest / len(split))
        gain = gain * jnp.repeat(jnp.exp(heights), extent[dim] // blocks).reshape((-1,) + (1,) * (len(extent) - 1 - dim))
    return gain


def centred(rng, extent, scale, reach, cuts=(), kind=jnp.bfloat16):
    entries = jax.random.normal(rng, extent, jnp.float32) * scale
    if len(cuts) > 0:
        entries = shard_levels(rng, extent, cuts, -0.22, 0.18) * entries
    return jnp.clip(entries, min=-reach, max=reach).astype(kind)


def setup_inputs(seed: int = 0) -> dict:
    streams_of = jax.random.split(jax.random.key(seed), 10)
    x_start = jnp.clip(jnp.exp(math.log(2.0) - 1.3862944 * jax.random.uniform(streams_of[0], (D,), jnp.float32) ** shard_levels(streams_of[0], (D,), ((0, 4),), -0.2, 0.2)), 0.5, 2.0)
    y_start = jnp.clip(jax.random.uniform(streams_of[1], (), jnp.float32, -1.0, 1.0), -1.0, 1.0)
    z_start = centred(streams_of[2], (D,), 0.5, 3.0, ((0, 4),), jnp.float32)
    increments = centred(streams_of[3], (STEPS, PATHS, D), 0.4472, 2.7, ((1, 8), (2, 4)), jnp.float32)
    default_step = with_ends(jax.random.randint(streams_of[4], (PATHS,), 0, STEPS + 2), jax.random.fold_in(streams_of[4], 1), 0, (STEPS + 2) - 1).astype(jnp.int32)
    term_weight = centred(streams_of[5], (D,), 1.0, 6.0, ((0, 4),), jnp.float32)
    w_first = centred(streams_of[6], (NETS, D, H), D ** -0.5, 0.1875, ((2, 4),))
    w_second = centred(streams_of[7], (NETS, H, H), H ** -0.5, 0.1875, ((1, 4),))
    w_third = centred(streams_of[8], (NETS, H, D), H ** -0.5, 0.1875, ((2, 4),))
    return {"x_start": x_start, "y_start": y_start, "z_start": z_start, "increments": increments, "default_step": default_step, "term_weight": term_weight, "w_first": w_first, "w_second": w_second, "w_third": w_third}


DRIFT_RATE = 0.06
VOLATILITY = 0.2
DISCOUNT = 0.02
DEFAULT_LOSS = 1.0 / 3.0

def reference(x_start, y_start, z_start, increments, default_step, term_weight, w_first, w_second, w_third):
    steps = increments.shape[0]
    tstep = 1.0 / steps
    paths = increments.shape[1]
    scale = 1.0 / math.sqrt(paths)
    counter = jnp.arange(steps, dtype=jnp.int32)
    factors = 1.0 + DISCOUNT * tstep - DEFAULT_LOSS * (counter[:, None] == default_step[None, :]).astype(jnp.float32)
    states = jnp.broadcast_to(x_start[None, :], (paths, x_start.shape[0]))
    dots = [lax.optimization_barrier(jnp.sum(increments[0] * z_start[None, :], axis=1))]
    states = states * (1.0 + DRIFT_RATE * tstep + VOLATILITY * increments[0])
    saved = []
    for index in range(1, steps):
        inputs_bf = states.astype(jnp.bfloat16)
        tanh_first = jnp.tanh(jnp.dot(inputs_bf, w_first[index - 1], preferred_element_type=jnp.float32))
        hidden_first = tanh_first.astype(jnp.bfloat16)
        tanh_second = jnp.tanh(jnp.dot(hidden_first, w_second[index - 1], preferred_element_type=jnp.float32))
        hidden_second = tanh_second.astype(jnp.bfloat16)
        control = jnp.dot(hidden_second, w_third[index - 1], preferred_element_type=jnp.float32)
        dots.append(lax.optimization_barrier(jnp.sum(control * increments[index], axis=1)))
        saved.append((inputs_bf, tanh_first, hidden_first, tanh_second, hidden_second))
        states = states * (1.0 + DRIFT_RATE * tstep + VOLATILITY * increments[index])
    target = lax.optimization_barrier(jnp.sum(states * term_weight[None, :], axis=1)) / math.sqrt(D)
    value = jnp.broadcast_to(y_start, (paths,)).astype(jnp.float32)
    for index in range(steps):
        value = factors[index] * value + dots[index]
    error = value - target
    loss = scale * jnp.sum(error * error)
    adjoint = 2.0 * scale * error
    firsts, seconds, thirds = ([], [], [])
    for index in range(steps - 1, 0, -1):
        inputs_bf, tanh_first, hidden_first, tanh_second, hidden_second = saved[index - 1]
        d_control = (adjoint[:, None] * increments[index]).astype(jnp.bfloat16)
        thirds.append(jnp.dot(hidden_second.T, d_control, preferred_element_type=jnp.float32))
        back_second = jnp.dot(d_control, w_third[index - 1].T, preferred_element_type=jnp.float32)
        d_second = (back_second * (1.0 - tanh_second * tanh_second)).astype(jnp.bfloat16)
        seconds.append(jnp.dot(hidden_first.T, d_second, preferred_element_type=jnp.float32))
        back_first = jnp.dot(d_second, w_second[index - 1].T, preferred_element_type=jnp.float32)
        d_first = (back_first * (1.0 - tanh_first * tanh_first)).astype(jnp.bfloat16)
        firsts.append(jnp.dot(inputs_bf.T, d_first, preferred_element_type=jnp.float32))
        adjoint = adjoint * factors[index]
    grad_z = lax.optimization_barrier(jnp.sum(adjoint[:, None] * increments[0], axis=0))
    adjoint = adjoint * factors[0]
    grad_y = jnp.sum(adjoint)
    grad_first = jnp.stack(firsts[::-1]).astype(jnp.bfloat16)
    grad_second = jnp.stack(seconds[::-1]).astype(jnp.bfloat16)
    grad_third = jnp.stack(thirds[::-1]).astype(jnp.bfloat16)
    return (loss, grad_y, grad_z, grad_first, grad_second, grad_third)
```

```python
import math

import jax
import jax.numpy as jnp
from jax import lax
from jax.sharding import PartitionSpec as P

D = 1024


DRIFT_RATE = 0.06
VOLATILITY = 0.2
DISCOUNT = 0.02
DEFAULT_LOSS = 1.0 / 3.0


def local_dense(
    x_start, y_start, z_start, increments, default_step, term_weight, w_first, w_second, w_third
):
    steps = increments.shape[0]
    tstep = 1.0 / steps
    local_paths = increments.shape[1]
    scale = 1.0 / math.sqrt(local_paths * lax.axis_size("batch"))
    counter = jnp.arange(steps, dtype=jnp.int32)
    factors = (
        1.0
        + DISCOUNT * tstep
        - DEFAULT_LOSS * (counter[:, None] == default_step[None, :]).astype(jnp.float32)
    )
    states = jnp.broadcast_to(x_start[None, :], (local_paths, x_start.shape[0]))
    partials = [jnp.sum(increments[0] * z_start[None, :], axis=1)]
    states = states * (1.0 + DRIFT_RATE * tstep + VOLATILITY * increments[0])
    saved = []
    for index in range(1, steps):
        inputs_bf = lax.all_gather(states.astype(jnp.bfloat16), "dim", axis=1, tiled=True)
        tanh_first = jnp.tanh(
            jnp.dot(inputs_bf, w_first[index - 1], preferred_element_type=jnp.float32)
        )
        hidden_first = tanh_first.astype(jnp.bfloat16)
        part_second = jnp.dot(hidden_first, w_second[index - 1], preferred_element_type=jnp.float32)
        tanh_second = jnp.tanh(
            lax.psum_scatter(part_second, "dim", scatter_dimension=1, tiled=True)
        )
        hidden_second = lax.all_gather(tanh_second.astype(jnp.bfloat16), "dim", axis=1, tiled=True)
        control = jnp.dot(hidden_second, w_third[index - 1], preferred_element_type=jnp.float32)
        partials.append(jnp.sum(control * increments[index], axis=1))
        saved.append((inputs_bf, tanh_first, hidden_first, tanh_second, hidden_second))
        states = states * (1.0 + DRIFT_RATE * tstep + VOLATILITY * increments[index])
    target_part = jnp.sum(states * term_weight[None, :], axis=1) / math.sqrt(D)
    value = jnp.broadcast_to(y_start, (local_paths,))
    for index in range(steps):
        value = factors[index] * value + lax.psum(partials[index], "dim")
    target = lax.psum(target_part, "dim")
    error = value - target
    loss_local = scale * jnp.sum(error * error)
    adjoint = 2.0 * scale * error
    firsts, seconds, thirds = ([], [], [])
    for index in range(steps - 1, 0, -1):
        inputs_bf, tanh_first, hidden_first, tanh_second, hidden_second = saved[index - 1]
        d_control = (adjoint[:, None] * increments[index]).astype(jnp.bfloat16)
        grad_out = jnp.dot(hidden_second.T, d_control, preferred_element_type=jnp.float32)
        back_part = jnp.dot(d_control, w_third[index - 1].T, preferred_element_type=jnp.float32)
        back_share = lax.psum_scatter(back_part, "dim", scatter_dimension=1, tiled=True)
        d_share = (back_share * (1.0 - tanh_second * tanh_second)).astype(jnp.bfloat16)
        d_second = lax.all_gather(d_share, "dim", axis=1, tiled=True)
        grad_mid = jnp.dot(hidden_first.T, d_second, preferred_element_type=jnp.float32)
        back_first = jnp.dot(d_second, w_second[index - 1].T, preferred_element_type=jnp.float32)
        d_first = (back_first * (1.0 - tanh_first * tanh_first)).astype(jnp.bfloat16)
        grad_in = jnp.dot(inputs_bf.T, d_first, preferred_element_type=jnp.float32)
        firsts.append(grad_in)
        seconds.append(grad_mid)
        thirds.append(grad_out)
        adjoint = adjoint * factors[index]
    grad_z_part = jnp.sum(adjoint[:, None] * increments[0], axis=0)
    adjoint = adjoint * factors[0]
    grad_y_part = jnp.sum(adjoint)
    stack_first = jnp.stack(firsts[::-1])
    stack_second = jnp.stack(seconds[::-1])
    stack_third = jnp.stack(thirds[::-1])
    loss, grad_y, grad_z, stack_first, stack_second, stack_third = lax.psum(
        (loss_local, grad_y_part, grad_z_part, stack_first, stack_second, stack_third), "batch"
    )
    return (
        loss,
        grad_y,
        grad_z,
        stack_first.astype(jnp.bfloat16),
        stack_second.astype(jnp.bfloat16),
        stack_third.astype(jnp.bfloat16),
    )


def swap(value):
    return lax.all_to_all(value, "dim", split_axis=0, concat_axis=0, tiled=True)


def local_nets(
    x_start, y_start, z_start, increments, default_step, term_weight, w_first, w_second, w_third
):
    f32, bf16 = jnp.float32, jnp.bfloat16
    steps, paths, share = increments.shape
    nets = steps - 1
    width = w_first.shape[1]
    hidden = w_second.shape[2]
    rows = lax.axis_size("batch")
    tstep = 1.0 / steps
    scale = 1.0 / math.sqrt(paths * rows)
    me = lax.axis_index("dim")
    counter = jnp.arange(steps, dtype=jnp.int32)
    factors = (
        1.0
        + DISCOUNT * tstep
        - DEFAULT_LOSS * (counter[:, None] == default_step[None, :]).astype(f32)
    )
    states = jnp.broadcast_to(x_start[None, :], (paths, share))
    dot_start = jnp.sum(increments[0] * z_start[None, :], axis=1)
    sent = []
    for index in range(steps):
        if index > 0:
            sent.append(states.astype(bf16))
        states = states * (1.0 + DRIFT_RATE * tstep + VOLATILITY * increments[index])
    target_part = jnp.sum(states * term_weight[None, :], axis=1) / math.sqrt(share * lax.axis_size("dim"))

    def whole(value):
        return jnp.transpose(swap(value), (1, 0, 2)).reshape(paths, width)

    inputs = whole(jnp.stack(sent))
    inc = whole(increments[1:])
    third = swap(w_third)
    first = swap(w_first)
    second = swap(w_second).reshape(hidden, hidden)
    first = jnp.transpose(first, (1, 0, 2)).reshape(width, hidden)
    third = jnp.transpose(third, (1, 0, 2)).reshape(hidden, width)
    high = inc.astype(bf16)
    low = (inc - high.astype(f32)).astype(bf16)
    back = jnp.dot(high, third.T, preferred_element_type=f32) + jnp.dot(
        low, third.T, preferred_element_type=f32
    )
    tanh_first = jnp.tanh(jnp.dot(inputs, first, preferred_element_type=f32))
    hidden_first = tanh_first.astype(bf16)
    tanh_second = jnp.tanh(jnp.dot(hidden_first, second, preferred_element_type=f32))
    hidden_second = tanh_second.astype(bf16)
    dot_mine = jnp.sum(hidden_second.astype(f32) * back, axis=1)
    slope_second = back * (1.0 - tanh_second * tanh_second)
    slope_first = jnp.dot(slope_second.astype(bf16), second.T, preferred_element_type=f32) * (
        1.0 - tanh_first * tanh_first
    )
    shared = lax.all_gather(jnp.stack([dot_mine, dot_start, target_part]), "dim")
    value = factors[0] * y_start + jnp.sum(shared[:, 1], axis=0)
    for index in range(1, steps):
        value = factors[index] * value + shared[index - 1, 0]
    error = value - jnp.sum(shared[:, 2], axis=0)
    loss_local = scale * jnp.sum(error * error)
    adjoint = 2.0 * scale * error
    adjoints = []
    for index in range(steps - 1, 0, -1):
        adjoints.append(adjoint)
        adjoint = adjoint * factors[index]
    grad_z_part = jnp.sum(adjoint[:, None] * increments[0], axis=0)
    grad_y_part = jnp.sum(adjoint * factors[0])
    mine = lax.dynamic_index_in_dim(jnp.stack(adjoints[::-1]), me, keepdims=False)[:, None]
    grad_third = jnp.dot(hidden_second.T, (mine * inc).astype(bf16), preferred_element_type=f32)
    grad_second = jnp.dot(
        hidden_first.T, (mine * slope_second).astype(bf16), preferred_element_type=f32
    )
    grad_first = jnp.dot(inputs.T, (mine * slope_first).astype(bf16), preferred_element_type=f32)

    def columns(grad):
        part = lax.psum_scatter(grad.astype(bf16), "batch", scatter_dimension=0, tiled=True)
        part = jnp.transpose(part.reshape(part.shape[0], nets, -1), (1, 0, 2))
        return lax.all_gather(swap(part), "batch", axis=1, tiled=True)

    def lines(grad):
        grad = grad.astype(bf16).reshape(nets, -1, grad.shape[1])
        part = lax.psum_scatter(grad, "batch", scatter_dimension=1, tiled=True)
        return lax.all_gather(swap(part), "batch", axis=1, tiled=True)

    loss, grad_y, grad_z = lax.psum((loss_local, grad_y_part, grad_z_part), "batch")
    return (
        loss,
        grad_y,
        grad_z,
        columns(grad_first),
        lines(grad_second),
        columns(grad_third),
    )


def pick(mesh):
    def run(*args):
        nets = args[6].shape[0]
        fits = mesh.shape["dim"] == nets
        return (local_nets if fits else local_dense)(*args)

    return run


def solution(mesh):
    placed = (
        P("dim"),
        P(),
        P("dim"),
        P(None, "batch", "dim"),
        P("batch"),
        P("dim"),
        P(None, None, "dim"),
        P(None, "dim", None),
        P(None, None, "dim"),
    )
    return jax.shard_map(
        pick(mesh),
        mesh=mesh,
        in_specs=placed,
        out_specs=(
            P(),
            P(),
            P("dim"),
            P(None, None, "dim"),
            P(None, "dim", None),
            P(None, None, "dim"),
        ),
        check_vma=False,
    )
```

```python
import functools
import math

import jax
import jax.numpy as jnp
from jax import lax
from jax.experimental import pallas as pl
from jax.experimental.pallas import tpu as pltpu
from jax.sharding import PartitionSpec as P

D = 1024


DRIFT_RATE = 0.06
VOLATILITY = 0.2
DISCOUNT = 0.02
DEFAULT_LOSS = 1.0 / 3.0


def local_dense(
    x_start, y_start, z_start, increments, default_step, term_weight, w_first, w_second, w_third
):
    steps = increments.shape[0]
    tstep = 1.0 / steps
    local_paths = increments.shape[1]
    scale = 1.0 / math.sqrt(local_paths * lax.axis_size("batch"))
    counter = jnp.arange(steps, dtype=jnp.int32)
    factors = (
        1.0
        + DISCOUNT * tstep
        - DEFAULT_LOSS * (counter[:, None] == default_step[None, :]).astype(jnp.float32)
    )
    states = jnp.broadcast_to(x_start[None, :], (local_paths, x_start.shape[0]))
    partials = [jnp.sum(increments[0] * z_start[None, :], axis=1)]
    states = states * (1.0 + DRIFT_RATE * tstep + VOLATILITY * increments[0])
    saved = []
    for index in range(1, steps):
        inputs_bf = lax.all_gather(states.astype(jnp.bfloat16), "dim", axis=1, tiled=True)
        tanh_first = jnp.tanh(
            jnp.dot(inputs_bf, w_first[index - 1], preferred_element_type=jnp.float32)
        )
        hidden_first = tanh_first.astype(jnp.bfloat16)
        part_second = jnp.dot(hidden_first, w_second[index - 1], preferred_element_type=jnp.float32)
        tanh_second = jnp.tanh(
            lax.psum_scatter(part_second, "dim", scatter_dimension=1, tiled=True)
        )
        hidden_second = lax.all_gather(tanh_second.astype(jnp.bfloat16), "dim", axis=1, tiled=True)
        control = jnp.dot(hidden_second, w_third[index - 1], preferred_element_type=jnp.float32)
        partials.append(jnp.sum(control * increments[index], axis=1))
        saved.append((inputs_bf, tanh_first, hidden_first, tanh_second, hidden_second))
        states = states * (1.0 + DRIFT_RATE * tstep + VOLATILITY * increments[index])
    target_part = jnp.sum(states * term_weight[None, :], axis=1) / math.sqrt(D)
    value = jnp.broadcast_to(y_start, (local_paths,))
    for index in range(steps):
        value = factors[index] * value + lax.psum(partials[index], "dim")
    target = lax.psum(target_part, "dim")
    error = value - target
    loss_local = scale * jnp.sum(error * error)
    adjoint = 2.0 * scale * error
    firsts, seconds, thirds = ([], [], [])
    for index in range(steps - 1, 0, -1):
        inputs_bf, tanh_first, hidden_first, tanh_second, hidden_second = saved[index - 1]
        d_control = (adjoint[:, None] * increments[index]).astype(jnp.bfloat16)
        grad_out = jnp.dot(hidden_second.T, d_control, preferred_element_type=jnp.float32)
        back_part = jnp.dot(d_control, w_third[index - 1].T, preferred_element_type=jnp.float32)
        back_share = lax.psum_scatter(back_part, "dim", scatter_dimension=1, tiled=True)
        d_share = (back_share * (1.0 - tanh_second * tanh_second)).astype(jnp.bfloat16)
        d_second = lax.all_gather(d_share, "dim", axis=1, tiled=True)
        grad_mid = jnp.dot(hidden_first.T, d_second, preferred_element_type=jnp.float32)
        back_first = jnp.dot(d_second, w_second[index - 1].T, preferred_element_type=jnp.float32)
        d_first = (back_first * (1.0 - tanh_first * tanh_first)).astype(jnp.bfloat16)
        grad_in = jnp.dot(inputs_bf.T, d_first, preferred_element_type=jnp.float32)
        firsts.append(grad_in)
        seconds.append(grad_mid)
        thirds.append(grad_out)
        adjoint = adjoint * factors[index]
    grad_z_part = jnp.sum(adjoint[:, None] * increments[0], axis=0)
    adjoint = adjoint * factors[0]
    grad_y_part = jnp.sum(adjoint)
    stack_first = jnp.stack(firsts[::-1])
    stack_second = jnp.stack(seconds[::-1])
    stack_third = jnp.stack(thirds[::-1])
    loss, grad_y, grad_z, stack_first, stack_second, stack_third = lax.psum(
        (loss_local, grad_y_part, grad_z_part, stack_first, stack_second, stack_third), "batch"
    )
    return (
        loss,
        grad_y,
        grad_z,
        stack_first.astype(jnp.bfloat16),
        stack_second.astype(jnp.bfloat16),
        stack_third.astype(jnp.bfloat16),
    )


MESH = pl.DeviceIdType.MESH
PAIR = 2


def remote(src, dst, sems, slot, target):
    return pltpu.make_async_remote_copy(
        src_ref=src,
        dst_ref=dst,
        send_sem=sems[0].at[slot],
        recv_sem=sems[1].at[slot],
        device_id=target,
        device_id_type=MESH,
    )


def greet(targets):
    barrier = pltpu.get_barrier_semaphore()
    for target in targets:
        pl.semaphore_signal(barrier, inc=1, device_id=target, device_id_type=MESH)
    pl.semaphore_wait(barrier, len(targets))


def fetch_kernel(nets, inc, state, third, first, second, inc_out, state_out, third_out, first_out, second_out, send, recv, far_send, far_recv, own):
    row, me = lax.axis_index("batch"), lax.axis_index("dim")
    side = lax.rem(row, PAIR)
    beside = {"batch": row + 1 - 2 * side}
    core, chip = lax.rem(me, PAIR), me // PAIR
    chips = nets // PAIR
    partner = chip * PAIR + 1 - core
    far = [
        (lax.rem(chip + jump, chips) * PAIR + lax.rem(core + turn, PAIR), lax.rem(chip + chips - jump, chips) * PAIR + lax.rem(core + turn, PAIR))
        for jump in range(1, chips)
        for turn in range(PAIR)
    ]
    share = inc.shape[2]
    greet([beside, {"dim": partner}] + [{"dim": ahead} for ahead, _ in far])

    def columns(source):
        return pl.ds(pl.multiple_of(source * share, share), share)

    def place(out, source, half, lines):
        if lines:
            depth = second.shape[1]
            if half is None:
                return out.at[pl.ds(pl.multiple_of(source * depth, depth), depth), :]
            cut = depth // PAIR
            return out.at[pl.ds(pl.multiple_of(source * depth + half * cut, cut), cut), :]
        if half is None:
            return out.at[:, columns(source)]
        cut = out.shape[0] // PAIR
        return out.at[pl.ds(pl.multiple_of(half * cut, cut), cut), columns(source)]

    def piece(value, target, half):
        if half is None:
            return value.at[target]
        cut = value.shape[1] // PAIR
        return value.at[target, pl.ds(pl.multiple_of(half * cut, cut), cut), :]

    whole = [(inc, inc_out), (state, state_out)]
    split = [(third, third_out, False), (first, first_out, False), (second, second_out, True)]
    every = [(value, out, False) for value, out in whole] + split
    waits, forwards = [], []
    slot = 0
    for value, out in whole:
        for ahead, _ in far:
            copy = remote(piece(value, ahead, None), place(out, me, None, False), (send, recv), slot, {"dim": ahead})
            copy.start()
            waits.append(copy)
            slot += 1
    for value, out, lines in split:
        for ahead, behind in far:
            copy = remote(piece(value, ahead, side), place(out, me, side, lines), (send, recv), slot, {"dim": ahead})
            copy.start()
            forwards.append((copy, out, behind, lines))
            slot += 1
    locals_ = []
    for index, (value, out, lines) in enumerate(every):
        copy = remote(piece(value, partner, None), place(out, me, None, lines), (send, recv), slot, {"dim": partner})
        copy.start()
        waits.append(copy)
        slot += 1
        copy = pltpu.make_async_copy(piece(value, me, None), place(out, me, None, lines), own.at[index])
        copy.start()
        locals_.append(copy)
    for index, (copy, out, behind, lines) in enumerate(forwards):
        copy.wait_recv()
        spot = place(out, behind, side, lines)
        onward = remote(spot, spot, (far_send, far_recv), index, beside)
        onward.start()
        waits.append(onward)
    for copy, _, _, _ in forwards:
        copy.wait_send()
    for copy in waits:
        copy.wait()
    for copy in locals_:
        copy.wait()


def fetch(inc, state, third, first, second):
    nets = third.shape[0]
    paths, width, hidden = inc.shape[1], first.shape[1], second.shape[2]
    away = nets - PAIR
    copies = 5 * away + 5
    any_spec = pl.BlockSpec(memory_space=pl.ANY)
    return pl.pallas_call(
        functools.partial(fetch_kernel, nets),
        out_shape=(
            jax.ShapeDtypeStruct((paths, width), inc.dtype),
            jax.ShapeDtypeStruct((paths, width), state.dtype),
            jax.ShapeDtypeStruct((hidden, width), third.dtype),
            jax.ShapeDtypeStruct((width, hidden), first.dtype),
            jax.ShapeDtypeStruct((hidden, hidden), second.dtype),
        ),
        in_specs=[pl.BlockSpec(memory_space=pltpu.VMEM)] * 5,
        out_specs=(any_spec,) * 5,
        scratch_shapes=[
            pltpu.SemaphoreType.DMA((copies,)),
            pltpu.SemaphoreType.DMA((copies,)),
            pltpu.SemaphoreType.DMA((3 * away,)),
            pltpu.SemaphoreType.DMA((3 * away,)),
            pltpu.SemaphoreType.DMA((5,)),
        ],
        compiler_params=pltpu.CompilerParams(
            collective_id=0, has_side_effects=True, vmem_limit_bytes=16 * 1024 * 1024
        ),
        name="fetch",
    )(inc, state, third, first, second)


def reduce_kernel(rows, nets, *refs):
    grads, small, outs, small_out = refs[0:3], refs[3], refs[4:7], refs[7]
    near, passed, landed, total = refs[8:11], refs[11:14], refs[14:17], refs[17:20]
    gathered = refs[20]
    near_sems, deep_sems, dim_sems, deep_out, near_out, small_sems = (
        (refs[21 + 2 * index], refs[22 + 2 * index]) for index in range(6)
    )
    own = refs[33]
    f32, bf16 = jnp.float32, jnp.bfloat16
    row, me = lax.axis_index("batch"), lax.axis_index("dim")
    side, level = lax.rem(row, PAIR), row // PAIR
    levels = rows // PAIR
    beside = {"batch": row + 1 - 2 * side}
    mats = range(3)
    cuts = [grad.shape[1] // rows for grad in grads]

    def at_level(jump):
        return lax.rem(level + jump + levels, levels)

    def lines(mat, owner):
        return pl.ds(pl.multiple_of(owner * cuts[mat], cuts[mat]), cuts[mat])

    greet(
        [{"batch": lax.rem(row + jump, rows)} for jump in range(1, rows)]
        + [{"dim": lax.rem(me + jump, nets)} for jump in range(1, nets)]
    )
    order = list(range(1, levels)) + [0]
    waits = []
    near_copies = {}
    for jump in order:
        for mat in mats:
            owner = at_level(jump) * PAIR + 1 - side
            copy = remote(
                grads[mat].at[:, lines(mat, owner), :], near[mat].at[jump], near_sems, jump * 3 + mat, beside
            )
            copy.start()
            near_copies[jump, mat] = copy
    small_copies = []
    for jump in range(1, rows):
        copy = remote(small, gathered.at[row], small_sems, jump - 1, {"batch": lax.rem(row + jump, rows)})
        copy.start()
        small_copies.append(copy)
    gathered[row] = small[...]
    deep_copies = {}
    for jump in order[:-1]:
        for mat in mats:
            near_copies[jump, mat].wait_recv()
            owner = at_level(jump) * PAIR + side
            both = grads[mat][:, lines(mat, owner), :].astype(f32) + near[mat][jump].astype(f32)
            passed[mat][jump - 1] = both.astype(bf16)
            copy = remote(
                passed[mat].at[jump - 1], landed[mat].at[jump - 1], deep_sems, (jump - 1) * 3 + mat,
                {"batch": owner},
            )
            copy.start()
            deep_copies[jump, mat] = copy
    dim_copies = {}
    for mat in mats:
        near_copies[0, mat].wait_recv()
        entire = grads[mat][:, lines(mat, row), :].astype(f32) + near[mat][0].astype(f32)
        for jump in order[:-1]:
            deep_copies[jump, mat].wait_recv()
            entire = entire + landed[mat][jump - 1].astype(f32)
        total[mat][...] = entire.astype(bf16)
        spot = outs[mat].at[me, lines(mat, row), :]
        for jump in range(1, nets):
            peer = lax.rem(me + jump, nets)
            copy = remote(total[mat].at[peer], spot, dim_sems, (jump - 1) * 3 + mat, {"dim": peer})
            copy.start()
            dim_copies[jump, mat] = copy
        copy = pltpu.make_async_copy(total[mat].at[me], spot, own.at[mat])
        copy.start()
        dim_copies[0, mat] = copy
    out_copies = {}
    for mat in mats:
        dim_copies[0, mat].wait()
        for jump in range(1, nets):
            dim_copies[jump, mat].wait_recv()
        spot = outs[mat].at[:, lines(mat, row), :]
        for jump in range(1, levels):
            copy = remote(
                spot, spot, deep_out, (jump - 1) * 3 + mat, {"batch": at_level(jump) * PAIR + side}
            )
            copy.start()
            out_copies[jump, mat] = copy
        copy = remote(spot, spot, near_out, mat, beside)
        copy.start()
        waits.append(copy)
    for jump in range(1, levels):
        for mat in mats:
            out_copies[jump, mat].wait_recv()
            spot = outs[mat].at[:, lines(mat, at_level(-jump) * PAIR + side), :]
            copy = remote(spot, spot, near_out, jump * 3 + mat, beside)
            copy.start()
            waits.append(copy)
    for copy in small_copies:
        copy.wait()
    summed = gathered[0]
    for index in range(1, rows):
        summed = summed + gathered[index]
    small_out[...] = summed
    for group in (near_copies, deep_copies, out_copies):
        for copy in group.values():
            copy.wait_send()
    for (jump, _), copy in dim_copies.items():
        if jump > 0:
            copy.wait_send()
    for copy in waits:
        copy.wait()


def reduce_grads(grads, small, rows):
    nets = grads[0].shape[0]
    levels = rows // PAIR
    bf16 = jnp.bfloat16
    any_spec = pl.BlockSpec(memory_space=pl.ANY)
    vmem = pl.BlockSpec(memory_space=pltpu.VMEM)

    def pieces(*count):
        return [
            pltpu.VMEM(count + (nets, grad.shape[1] // rows, grad.shape[2]), bf16) for grad in grads
        ]

    def dma(count):
        return [pltpu.SemaphoreType.DMA((count,))] * 2

    return pl.pallas_call(
        functools.partial(reduce_kernel, rows, nets),
        out_shape=tuple(jax.ShapeDtypeStruct(grad.shape, bf16) for grad in grads)
        + (jax.ShapeDtypeStruct(small.shape, small.dtype),),
        in_specs=[vmem] * 4,
        out_specs=(any_spec,) * 3 + (vmem,),
        scratch_shapes=pieces(levels)
        + pieces(levels - 1)
        + pieces(levels - 1)
        + pieces()
        + [pltpu.VMEM((rows,) + small.shape, small.dtype)]
        + dma(3 * levels)
        + dma(3 * (levels - 1))
        + dma(3 * (nets - 1))
        + dma(3 * (levels - 1))
        + dma(3 * levels)
        + dma(rows - 1)
        + [pltpu.SemaphoreType.DMA((3,))],
        compiler_params=pltpu.CompilerParams(
            collective_id=1, has_side_effects=True, vmem_limit_bytes=32 * 1024 * 1024
        ),
        name="reduce_grads",
    )(*grads, small)


def local_nets(
    x_start, y_start, z_start, increments, default_step, term_weight, w_first, w_second, w_third
):
    f32, bf16 = jnp.float32, jnp.bfloat16
    steps, paths, share = increments.shape
    nets = steps - 1
    width = w_first.shape[1]
    hidden = w_second.shape[2]
    rows = lax.axis_size("batch")
    tstep = 1.0 / steps
    scale = 1.0 / math.sqrt(paths * rows)
    me = lax.axis_index("dim")
    counter = jnp.arange(steps, dtype=jnp.int32)
    factors = (
        1.0
        + DISCOUNT * tstep
        - DEFAULT_LOSS * (counter[:, None] == default_step[None, :]).astype(f32)
    )
    states = jnp.broadcast_to(x_start[None, :], (paths, share))
    dot_start = jnp.sum(increments[0] * z_start[None, :], axis=1)
    sent = []
    for index in range(steps):
        if index > 0:
            sent.append(states.astype(bf16))
        states = states * (1.0 + DRIFT_RATE * tstep + VOLATILITY * increments[index])
    target_part = jnp.sum(states * term_weight[None, :], axis=1) / math.sqrt(share * lax.axis_size("dim"))

    inc, inputs, third, first, second = fetch(
        increments[1:], jnp.stack(sent), w_third, w_first, w_second
    )
    high = inc.astype(bf16)
    low = (inc - high.astype(f32)).astype(bf16)
    back = jnp.dot(high, third.T, preferred_element_type=f32) + jnp.dot(
        low, third.T, preferred_element_type=f32
    )
    tanh_first = jnp.tanh(jnp.dot(inputs, first, preferred_element_type=f32))
    hidden_first = tanh_first.astype(bf16)
    tanh_second = jnp.tanh(jnp.dot(hidden_first, second, preferred_element_type=f32))
    hidden_second = tanh_second.astype(bf16)
    dot_mine = jnp.sum(hidden_second.astype(f32) * back, axis=1)
    slope_second = back * (1.0 - tanh_second * tanh_second)
    slope_first = jnp.dot(slope_second.astype(bf16), second.T, preferred_element_type=f32) * (
        1.0 - tanh_first * tanh_first
    )
    shared = lax.all_gather(jnp.stack([dot_mine, dot_start, target_part]), "dim")
    value = factors[0] * y_start + jnp.sum(shared[:, 1], axis=0)
    for index in range(1, steps):
        value = factors[index] * value + shared[index - 1, 0]
    error = value - jnp.sum(shared[:, 2], axis=0)
    loss_local = scale * jnp.sum(error * error)
    adjoint = 2.0 * scale * error
    adjoints = []
    for index in range(steps - 1, 0, -1):
        adjoints.append(adjoint)
        adjoint = adjoint * factors[index]
    grad_z_part = jnp.sum(adjoint[:, None] * increments[0], axis=0)
    grad_y_part = jnp.sum(adjoint * factors[0])
    mine = lax.dynamic_index_in_dim(jnp.stack(adjoints[::-1]), me, keepdims=False)[:, None]

    def columns(left, right):
        left = left.T
        blocks = jnp.split(right, nets, axis=1)
        return jnp.stack(
            [jnp.dot(left, block, preferred_element_type=f32).astype(bf16) for block in blocks]
        )

    grad_third = columns(hidden_second, (mine * inc).astype(bf16))
    grad_second = jnp.dot(
        hidden_first.T, (mine * slope_second).astype(bf16), preferred_element_type=f32
    ).astype(bf16)
    grad_first = columns(inputs, (mine * slope_first).astype(bf16))
    small = jnp.zeros((8, share), f32)
    small = small.at[0].set(grad_z_part).at[1].set(loss_local).at[2].set(grad_y_part)
    grad_first, grad_second, grad_third, small = reduce_grads(
        (grad_first, grad_second.reshape(nets, -1, hidden), grad_third), small, rows
    )
    return small[1, 0], small[2, 0], small[0], grad_first, grad_second, grad_third


def pick(mesh):
    def run(*args):
        nets = args[6].shape[0]
        fits = mesh.shape["dim"] == nets and nets % PAIR == 0 and mesh.shape["batch"] % PAIR == 0
        return (local_nets if fits else local_dense)(*args)

    return run


def solution(mesh):
    placed = (
        P("dim"),
        P(),
        P("dim"),
        P(None, "batch", "dim"),
        P("batch"),
        P("dim"),
        P(None, None, "dim"),
        P(None, "dim", None),
        P(None, None, "dim"),
    )
    return jax.shard_map(
        pick(mesh),
        mesh=mesh,
        in_specs=placed,
        out_specs=(
            P(),
            P(),
            P("dim"),
            P(None, None, "dim"),
            P(None, "dim", None),
            P(None, None, "dim"),
        ),
        check_vma=False,
    )
```

```python
import functools
import math

import jax
import jax.numpy as jnp
from jax import lax
from jax.experimental import pallas as pl
from jax.experimental.pallas import tpu as pltpu
from jax.sharding import PartitionSpec as P

D = 1024


DRIFT_RATE = 0.06
VOLATILITY = 0.2
DISCOUNT = 0.02
DEFAULT_LOSS = 1.0 / 3.0


def local_dense(
    x_start, y_start, z_start, increments, default_step, term_weight, w_first, w_second, w_third
):
    steps = increments.shape[0]
    tstep = 1.0 / steps
    local_paths = increments.shape[1]
    scale = 1.0 / math.sqrt(local_paths * lax.axis_size("batch"))
    counter = jnp.arange(steps, dtype=jnp.int32)
    factors = (
        1.0
        + DISCOUNT * tstep
        - DEFAULT_LOSS * (counter[:, None] == default_step[None, :]).astype(jnp.float32)
    )
    states = jnp.broadcast_to(x_start[None, :], (local_paths, x_start.shape[0]))
    partials = [jnp.sum(increments[0] * z_start[None, :], axis=1)]
    states = states * (1.0 + DRIFT_RATE * tstep + VOLATILITY * increments[0])
    saved = []
    for index in range(1, steps):
        inputs_bf = lax.all_gather(states.astype(jnp.bfloat16), "dim", axis=1, tiled=True)
        tanh_first = jnp.tanh(
            jnp.dot(inputs_bf, w_first[index - 1], preferred_element_type=jnp.float32)
        )
        hidden_first = tanh_first.astype(jnp.bfloat16)
        part_second = jnp.dot(hidden_first, w_second[index - 1], preferred_element_type=jnp.float32)
        tanh_second = jnp.tanh(
            lax.psum_scatter(part_second, "dim", scatter_dimension=1, tiled=True)
        )
        hidden_second = lax.all_gather(tanh_second.astype(jnp.bfloat16), "dim", axis=1, tiled=True)
        control = jnp.dot(hidden_second, w_third[index - 1], preferred_element_type=jnp.float32)
        partials.append(jnp.sum(control * increments[index], axis=1))
        saved.append((inputs_bf, tanh_first, hidden_first, tanh_second, hidden_second))
        states = states * (1.0 + DRIFT_RATE * tstep + VOLATILITY * increments[index])
    target_part = jnp.sum(states * term_weight[None, :], axis=1) / math.sqrt(D)
    value = jnp.broadcast_to(y_start, (local_paths,))
    for index in range(steps):
        value = factors[index] * value + lax.psum(partials[index], "dim")
    target = lax.psum(target_part, "dim")
    error = value - target
    loss_local = scale * jnp.sum(error * error)
    adjoint = 2.0 * scale * error
    firsts, seconds, thirds = ([], [], [])
    for index in range(steps - 1, 0, -1):
        inputs_bf, tanh_first, hidden_first, tanh_second, hidden_second = saved[index - 1]
        d_control = (adjoint[:, None] * increments[index]).astype(jnp.bfloat16)
        grad_out = jnp.dot(hidden_second.T, d_control, preferred_element_type=jnp.float32)
        back_part = jnp.dot(d_control, w_third[index - 1].T, preferred_element_type=jnp.float32)
        back_share = lax.psum_scatter(back_part, "dim", scatter_dimension=1, tiled=True)
        d_share = (back_share * (1.0 - tanh_second * tanh_second)).astype(jnp.bfloat16)
        d_second = lax.all_gather(d_share, "dim", axis=1, tiled=True)
        grad_mid = jnp.dot(hidden_first.T, d_second, preferred_element_type=jnp.float32)
        back_first = jnp.dot(d_second, w_second[index - 1].T, preferred_element_type=jnp.float32)
        d_first = (back_first * (1.0 - tanh_first * tanh_first)).astype(jnp.bfloat16)
        grad_in = jnp.dot(inputs_bf.T, d_first, preferred_element_type=jnp.float32)
        firsts.append(grad_in)
        seconds.append(grad_mid)
        thirds.append(grad_out)
        adjoint = adjoint * factors[index]
    grad_z_part = jnp.sum(adjoint[:, None] * increments[0], axis=0)
    adjoint = adjoint * factors[0]
    grad_y_part = jnp.sum(adjoint)
    stack_first = jnp.stack(firsts[::-1])
    stack_second = jnp.stack(seconds[::-1])
    stack_third = jnp.stack(thirds[::-1])
    loss, grad_y, grad_z, stack_first, stack_second, stack_third = lax.psum(
        (loss_local, grad_y_part, grad_z_part, stack_first, stack_second, stack_third), "batch"
    )
    return (
        loss,
        grad_y,
        grad_z,
        stack_first.astype(jnp.bfloat16),
        stack_second.astype(jnp.bfloat16),
        stack_third.astype(jnp.bfloat16),
    )


MESH = pl.DeviceIdType.MESH
PAIR = 2


def remote(src, dst, sems, slot, target):
    return pltpu.make_async_remote_copy(
        src_ref=src,
        dst_ref=dst,
        send_sem=sems[0].at[slot],
        recv_sem=sems[1].at[slot],
        device_id=target,
        device_id_type=MESH,
    )


def greet(targets):
    barrier = pltpu.get_barrier_semaphore()
    for target in targets:
        pl.semaphore_signal(barrier, inc=1, device_id=target, device_id_type=MESH)
    pl.semaphore_wait(barrier, len(targets))


def flip(bit, turn):
    return 1 - bit if turn else bit


def here():
    row, me = lax.axis_index("batch"), lax.axis_index("dim")
    return row // PAIR, lax.rem(row, PAIR), me // PAIR, lax.rem(me, PAIR)


def device(level, side, chip, core):
    return {"batch": level * PAIR + side, "dim": chip * PAIR + core}


def hop(level, bit):
    low, high = lax.rem(level, PAIR), level // PAIR
    return flip(high, bit == 1) * PAIR + flip(low, bit == 0)


FLIPS = [(up, across, turn) for up in range(2) for across in range(2) for turn in range(2)]


def fetch_kernel(inc, state, third, first, second, inc_out, state_out, third_out, first_out, second_out, *sems):
    path_sems, core_sems, chip_sems, level_sems, pass_sems, last_sems = (
        (sems[2 * index], sems[2 * index + 1]) for index in range(6)
    )
    own, own_path = sems[12], sems[13]
    level, side, chip, core = here()
    me = chip * PAIR + core
    net = chip * PAIR + side
    across = (1 - chip) * PAIR + core
    partner = device(level, side, chip, 1 - core)
    beyond = device(level, side, 1 - chip, core)
    above = device(hop(level, 0), side, chip, core)
    half = lax.rem(level, PAIR)
    share, depth = inc.shape[2], second.shape[1]
    greet(
        [device(level, flip(side, up), flip(chip, ac), flip(core, turn)) for up, ac, turn in FLIPS[1:]]
        + [above]
    )

    def columns(source):
        return pl.ds(pl.multiple_of(source * share, share), share)

    def place(out, source, lines, part):
        if lines:
            cut = depth if part is None else depth // PAIR
            start = source * depth if part is None else source * depth + part * cut
            return out.at[pl.ds(pl.multiple_of(start, cut), cut), :]
        if part is None:
            return out.at[:, columns(source)]
        cut = out.shape[0] // PAIR
        return out.at[pl.ds(pl.multiple_of(part * cut, cut), cut), columns(source)]

    mats = [(third, third_out, False), (first, first_out, False), (second, second_out, True)]
    paths = [(inc, inc_out), (state, state_out)]

    def path_copy(index, up, ac):
        value, out = paths[index]
        to_chip, to_side = flip(chip, ac), flip(side, up)
        slot = ((index * 2 + up) * 2 + ac) * PAIR + core
        return remote(
            value.at[to_chip * PAIR + to_side], out.at[:, columns(me)], path_sems, slot,
            device(level, to_side, to_chip, side),
        )

    def path_arrival(index, up, ac, source):
        value, out = paths[index]
        slot = ((index * 2 + up) * 2 + ac) * PAIR + source
        return remote(value.at[0], out.at[:, columns(me)], path_sems, slot, partner)

    def path_own(index):
        value, out = paths[index]
        return pltpu.make_async_copy(value.at[net], out.at[:, columns(me)], own_path.at[index])

    aligned = core == side
    for index in range(2):
        for up, ac in ((0, 1), (1, 1), (1, 0)):
            path_copy(index, up, ac).start()
    chip_copies, waits = [], []
    for index, (value, out, lines) in enumerate(mats):
        cut = value.shape[1] // PAIR
        copy = remote(
            value.at[(1 - chip) * PAIR + side, pl.ds(pl.multiple_of(half * cut, cut), cut), :],
            place(out, me, lines, half), chip_sems, index, beyond,
        )
        copy.start()
        chip_copies.append(copy)

    @pl.when(aligned)
    def _():
        for index in range(2):
            path_own(index).start()

    @pl.when(jnp.logical_not(aligned))
    def _():
        for index in range(2):
            path_copy(index, 0, 0).start()

    for index, (value, out, lines) in enumerate(mats):
        copy = remote(value.at[net], place(out, me, lines, None), core_sems, index, partner)
        copy.start()
        waits.append(copy)
        copy = pltpu.make_async_copy(value.at[net], place(out, me, lines, None), own.at[index])
        copy.start()
        waits.append(copy)
    level_copies = []
    for index, (value, out, lines) in enumerate(mats):
        chip_copies[index].wait_recv()
        spot = place(out, across, lines, half)
        copy = remote(spot, spot, level_sems, index, above)
        copy.start()
        level_copies.append(copy)
        copy = remote(spot, spot, pass_sems, index, partner)
        copy.start()
        waits.append(copy)
    for index, (value, out, lines) in enumerate(mats):
        level_copies[index].wait_recv()
        spot = place(out, across, lines, 1 - half)
        copy = remote(spot, spot, last_sems, index, partner)
        copy.start()
        waits.append(copy)
    for copy in chip_copies + level_copies:
        copy.wait_send()
    for index in range(2):
        for up, ac in ((0, 1), (1, 1), (1, 0)):
            path_copy(index, up, ac).wait_send()

    @pl.when(aligned)
    def _():
        for index in range(2):
            path_own(index).wait()
            path_arrival(index, 0, 0, 1 - core).wait_recv()
            for source in range(PAIR):
                path_arrival(index, 0, 1, source).wait_recv()

    @pl.when(jnp.logical_not(aligned))
    def _():
        for index in range(2):
            path_copy(index, 0, 0).wait_send()
            for ac in range(2):
                for source in range(PAIR):
                    path_arrival(index, 1, ac, source).wait_recv()

    for copy in waits:
        copy.wait()


def fetch(inc, state, third, first, second):
    nets = third.shape[0]
    paths, width, hidden = inc.shape[1], first.shape[1], second.shape[2]
    any_spec = pl.BlockSpec(memory_space=pl.ANY)
    counts = [4 * nets, 3, 3, 3, 3, 3]
    return pl.pallas_call(
        fetch_kernel,
        out_shape=(
            jax.ShapeDtypeStruct((paths, width), inc.dtype),
            jax.ShapeDtypeStruct((paths, width), state.dtype),
            jax.ShapeDtypeStruct((hidden, width), third.dtype),
            jax.ShapeDtypeStruct((width, hidden), first.dtype),
            jax.ShapeDtypeStruct((hidden, hidden), second.dtype),
        ),
        in_specs=[pl.BlockSpec(memory_space=pltpu.VMEM)] * 5,
        out_specs=(any_spec,) * 5,
        scratch_shapes=[pltpu.SemaphoreType.DMA((count,)) for count in counts for _ in range(2)]
        + [pltpu.SemaphoreType.DMA((3,)), pltpu.SemaphoreType.DMA((2,))],
        compiler_params=pltpu.CompilerParams(
            collective_id=0, has_side_effects=True, vmem_limit_bytes=16 * 1024 * 1024
        ),
        name="fetch",
    )(inc, state, third, first, second)


def share_kernel(block, out, gathered, send, recv):
    level, side, chip, core = here()
    targets = [device(level, flip(side, up), flip(chip, ac), flip(core, turn)) for up, ac, turn in FLIPS[1:]]
    greet(targets)
    copies = []
    for index, target in enumerate(targets):
        copy = remote(block, gathered.at[side, chip * PAIR + core], (send, recv), index, target)
        copy.start()
        copies.append(copy)
    gathered[side, chip * PAIR + core] = block[...]
    for copy in copies:
        copy.wait()
    out[...] = gathered[...]


def share_level(block, nets):
    shape = (PAIR, nets) + block.shape
    vmem = pl.BlockSpec(memory_space=pltpu.VMEM)
    return pl.pallas_call(
        share_kernel,
        out_shape=jax.ShapeDtypeStruct(shape, block.dtype),
        in_specs=[vmem],
        out_specs=vmem,
        scratch_shapes=[pltpu.VMEM(shape, block.dtype)]
        + [pltpu.SemaphoreType.DMA((len(FLIPS) - 1,))] * 2,
        compiler_params=pltpu.CompilerParams(collective_id=2, has_side_effects=True),
        name="share_level",
    )(block)


def reduce_kernel(rows, nets, *refs):
    grads, small, outs, small_out = refs[0:3], refs[3], refs[4:7], refs[7]
    zero, one, two = refs[8:11], refs[11:14], refs[14:17]
    sent_one, sent_two, held = refs[17:20], refs[20:23], refs[23:26]
    gathered = refs[26]
    zero_sems, one_sems, two_sems, back_two, back_one, out_sems, small_sems = (
        (refs[27 + 2 * index], refs[28 + 2 * index]) for index in range(7)
    )
    own = refs[41]
    f32, bf16 = jnp.float32, jnp.bfloat16
    level, side, chip, core = here()
    row = level * PAIR + side
    net = chip * PAIR + side
    low, high = lax.rem(level, PAIR), level // PAIR
    slot_mine = low * PAIR + high
    partner = device(level, side, chip, 1 - core)
    first, second = (device(hop(level, bit), side, chip, core) for bit in range(2))
    mats = range(3)
    cuts = [grad.shape[1] // rows for grad in grads]
    chunks = [(mat, turn) for turn in (1, 0) for mat in (2, 1, 0)]
    others = [(up, ac, turn) for up, ac, turn in FLIPS if (up, ac, turn) != (0, 0, 0)]
    greet(
        [{"batch": lax.rem(row + jump, rows)} for jump in range(1, rows)]
        + [device(level, flip(side, up), flip(chip, ac), flip(core, turn)) for up, ac, turn in others if ac or turn]
    )

    def shards(turn):
        return pl.ds(flip(chip, turn) * PAIR, PAIR)

    def span(mat, start, count):
        return pl.ds(pl.multiple_of(start * cuts[mat], cuts[mat]), count * cuts[mat])

    copies = {}

    def core_step(index):
        mat, turn = chunks[index]
        copy = remote(
            grads[mat].at[shards(turn), span(mat, (1 - core) * 4, 4), :],
            zero[mat].at[shards(turn)], zero_sems, index, partner,
        )
        copy.start()
        copies["zero", index] = copy

    def low_step(index):
        mat, turn = chunks[index]
        copies["zero", index].wait_recv()
        start = (1 - low) * 2
        value = grads[mat][shards(turn), span(mat, core * 4 + start, 2), :].astype(f32)
        value = value + zero[mat][shards(turn), span(mat, start, 2), :].astype(f32)
        sent_one[mat][shards(turn)] = value.astype(bf16)
        copy = remote(
            sent_one[mat].at[shards(turn)], one[mat].at[shards(turn)], one_sems, index, first
        )
        copy.start()
        copies["one", index] = copy

    def partial(mat, turn, end):
        value = grads[mat][shards(turn), span(mat, core * 4 + low * 2 + end, 1), :].astype(f32)
        value = value + zero[mat][shards(turn), span(mat, low * 2 + end, 1), :].astype(f32)
        return value + one[mat][shards(turn), span(mat, end, 1), :].astype(f32)

    def high_step(index):
        mat, turn = chunks[index]
        copies["one", index].wait_recv()
        sent_two[mat][shards(turn)] = partial(mat, turn, 1 - high).astype(bf16)
        copy = remote(
            sent_two[mat].at[shards(turn)], two[mat].at[shards(turn)], two_sems, index, second
        )
        copy.start()
        copies["two", index] = copy

    def spread(index, event, slot, count):
        mat, turn = chunks[index]
        lines = span(mat, core * 4 + slot, count)
        for up in range(2):
            for swapped in range(2):
                shard = flip(chip, turn) * PAIR + flip(core, swapped)
                src = held[mat].at[shard, span(mat, slot, count), :]
                dst = outs[mat].at[net, lines, :]
                if up or turn or swapped:
                    number = ((index * 3 + event) * 2 + up) * 2 + swapped
                    copy = remote(
                        src, dst, out_sems, number,
                        device(level, flip(side, up), flip(chip, turn), flip(core, swapped)),
                    )
                else:
                    copy = pltpu.make_async_copy(src, dst, own.at[index * 3 + event])
                copy.start()
                copies["out", index, event, up, swapped] = copy

    def final_step(index):
        mat, turn = chunks[index]
        copies["two", index].wait_recv()
        value = partial(mat, turn, high) + two[mat][shards(turn)].astype(f32)
        held[mat][shards(turn), span(mat, slot_mine, 1), :] = value.astype(bf16)
        spot = held[mat].at[shards(turn), span(mat, slot_mine, 1), :]
        for name, sems, target in (("back_two", back_two, second), ("back_one", back_one, first)):
            copy = remote(spot, spot, sems, index * 2 if name == "back_one" else index, target)
            copy.start()
            copies[name, index] = copy
        spread(index, 0, slot_mine, 1)

    def gather_step(index):
        mat, turn = chunks[index]
        copies["back_two", index].wait_recv()
        slot = low * PAIR + 1 - high
        spot = held[mat].at[shards(turn), span(mat, slot, 1), :]
        copy = remote(spot, spot, back_one, index * 2 + 1, first)
        copy.start()
        copies["back_far", index] = copy
        spread(index, 1, slot, 1)

    def last_step(index):
        copies["back_one", index].wait_recv()
        copies["back_far", index].wait_recv()
        spread(index, 2, (1 - low) * PAIR, PAIR)

    for index in range(len(chunks)):
        core_step(index)
    small_copies = []
    for jump in range(1, rows):
        copy = remote(small, gathered.at[row], small_sems, jump - 1, {"batch": lax.rem(row + jump, rows)})
        copy.start()
        small_copies.append(copy)
    gathered[row] = small[...]
    stages = (low_step, high_step, final_step, gather_step, last_step)
    for time in range(len(chunks) + len(stages) - 1):
        for lag in reversed(range(len(stages))):
            if 0 <= time - lag < len(chunks):
                stages[lag](time - lag)
    for copy in small_copies:
        copy.wait()
    summed = gathered[0]
    for index in range(1, rows):
        summed = summed + gathered[index]
    small_out[...] = summed
    for name, copy in copies.items():
        if name[0] == "out":
            copy.wait()
        else:
            copy.wait_send()


def reduce_grads(grads, small, rows):
    nets = grads[0].shape[0]
    bf16 = jnp.bfloat16
    any_spec = pl.BlockSpec(memory_space=pl.ANY)
    vmem = pl.BlockSpec(memory_space=pltpu.VMEM)
    chunks = 3 * PAIR

    def pieces(count):
        return [
            pltpu.VMEM((nets, count * (grad.shape[1] // rows), grad.shape[2]), bf16)
            for grad in grads
        ]

    def dma(count):
        return [pltpu.SemaphoreType.DMA((count,))] * 2

    return pl.pallas_call(
        functools.partial(reduce_kernel, rows, nets),
        out_shape=tuple(jax.ShapeDtypeStruct(grad.shape, bf16) for grad in grads)
        + (jax.ShapeDtypeStruct(small.shape, small.dtype),),
        in_specs=[vmem] * 4,
        out_specs=(any_spec,) * 3 + (vmem,),
        scratch_shapes=pieces(4)
        + pieces(2)
        + pieces(1)
        + pieces(2)
        + pieces(1)
        + pieces(4)
        + [pltpu.VMEM((rows,) + small.shape, small.dtype)]
        + dma(chunks)
        + dma(chunks)
        + dma(chunks)
        + dma(chunks)
        + dma(chunks * 2)
        + dma(chunks * 12)
        + dma(rows - 1)
        + [pltpu.SemaphoreType.DMA((chunks * 3,))],
        compiler_params=pltpu.CompilerParams(
            collective_id=1, has_side_effects=True, vmem_limit_bytes=36 * 1024 * 1024
        ),
        name="reduce_grads",
    )(*grads, small)


def local_nets(
    x_start, y_start, z_start, increments, default_step, term_weight, w_first, w_second, w_third
):
    f32, bf16 = jnp.float32, jnp.bfloat16
    steps, paths, share = increments.shape
    nets = steps - 1
    width = w_first.shape[1]
    hidden = w_second.shape[2]
    rows = lax.axis_size("batch")
    tstep = 1.0 / steps
    scale = 1.0 / math.sqrt(paths * rows)
    me = lax.axis_index("dim")
    counter = jnp.arange(steps, dtype=jnp.int32)
    states = jnp.broadcast_to(x_start[None, :], (paths, share))
    dot_start = jnp.sum(increments[0] * z_start[None, :], axis=1)
    sent = []
    for index in range(steps):
        if index > 0:
            sent.append(states.astype(bf16))
        states = states * (1.0 + DRIFT_RATE * tstep + VOLATILITY * increments[index])
    target_part = jnp.sum(states * term_weight[None, :], axis=1) / math.sqrt(share * lax.axis_size("dim"))

    inc, inputs, third, first, second = fetch(
        increments[1:], jnp.stack(sent), w_third, w_first, w_second
    )
    high = inc.astype(bf16)
    low = (inc - high.astype(f32)).astype(bf16)
    back = jnp.dot(high, third.T, preferred_element_type=f32) + jnp.dot(
        low, third.T, preferred_element_type=f32
    )
    tanh_first = jnp.tanh(jnp.dot(inputs, first, preferred_element_type=f32))
    hidden_first = tanh_first.astype(bf16)
    tanh_second = jnp.tanh(jnp.dot(hidden_first, second, preferred_element_type=f32))
    hidden_second = tanh_second.astype(bf16)
    dot_mine = jnp.sum(hidden_second.astype(f32) * back, axis=1)
    slope_second = back * (1.0 - tanh_second * tanh_second)
    slope_first = jnp.dot(slope_second.astype(bf16), second.T, preferred_element_type=f32) * (
        1.0 - tanh_first * tanh_first
    )
    block = jnp.zeros((8, paths), f32)
    block = block.at[0].set(dot_mine).at[1].set(dot_start).at[2].set(target_part)
    block = block.at[3].set(default_step.astype(f32))
    shared = share_level(block, nets)
    side, core = lax.rem(lax.axis_index("batch"), PAIR), lax.rem(me, PAIR)
    net = me // PAIR * PAIR + side
    falls = shared[:, 0, 3]
    factors = (
        1.0
        + DISCOUNT * tstep
        - DEFAULT_LOSS * (counter[:, None, None].astype(f32) == falls[None]).astype(f32)
    )
    value = factors[0] * y_start + jnp.sum(shared[:, :, 1], axis=1)
    for index in range(1, steps):
        chip, low = divmod(index - 1, PAIR)
        dots = shared[low, chip * PAIR : (chip + 1) * PAIR, 0]
        value = factors[index] * value + dots
    error = value - jnp.sum(shared[:, :, 2], axis=1)
    adjoint = 2.0 * scale * error
    adjoints = []
    for index in range(steps - 1, 0, -1):
        adjoints.append(adjoint)
        adjoint = adjoint * factors[index]
    start = lax.dynamic_index_in_dim(adjoint, side, keepdims=False)
    grad_z_part = jnp.sum(start[:, None] * increments[0], axis=0)
    grad_y_part = jnp.sum(start * lax.dynamic_index_in_dim(factors[0], side, keepdims=False))
    fault = lax.dynamic_index_in_dim(error, side, keepdims=False)
    loss_local = scale * jnp.sum(fault * fault)
    mine = lax.dynamic_index_in_dim(jnp.stack(adjoints[::-1]), net, keepdims=False)
    mine = lax.dynamic_index_in_dim(mine, core, keepdims=False)[:, None]

    def columns(left, right):
        left = left.T
        blocks = jnp.split(right, nets, axis=1)
        return jnp.stack(
            [jnp.dot(left, block, preferred_element_type=f32).astype(bf16) for block in blocks]
        )

    grad_third = columns(hidden_second, (mine * inc).astype(bf16))
    grad_second = jnp.dot(
        hidden_first.T, (mine * slope_second).astype(bf16), preferred_element_type=f32
    ).astype(bf16)
    grad_first = columns(inputs, (mine * slope_first).astype(bf16))
    small = jnp.zeros((8, share), f32)
    small = small.at[0].set(grad_z_part).at[1].set(loss_local).at[2].set(grad_y_part)
    grad_first, grad_second, grad_third, small = reduce_grads(
        (grad_first, grad_second.reshape(nets, -1, hidden), grad_third), small, rows
    )
    return small[1, 0], small[2, 0], small[0], grad_first, grad_second, grad_third


def pick(mesh):
    def run(*args):
        nets = args[6].shape[0]
        rows = mesh.shape["batch"]
        fits = mesh.shape["dim"] == nets == PAIR * PAIR and rows == PAIR * PAIR * PAIR
        return (local_nets if fits else local_dense)(*args)

    return run


def solution(mesh):
    placed = (
        P("dim"),
        P(),
        P("dim"),
        P(None, "batch", "dim"),
        P("batch"),
        P("dim"),
        P(None, None, "dim"),
        P(None, "dim", None),
        P(None, None, "dim"),
    )
    return jax.shard_map(
        pick(mesh),
        mesh=mesh,
        in_specs=placed,
        out_specs=(
            P(),
            P(),
            P("dim"),
            P(None, None, "dim"),
            P(None, "dim", None),
            P(None, None, "dim"),
        ),
        check_vma=False,
    )
```

```python
import functools
import math

import jax
import jax.numpy as jnp
from jax import lax
from jax.experimental import pallas as pl
from jax.experimental.pallas import tpu as pltpu
from jax.sharding import PartitionSpec as P

D = 1024


DRIFT_RATE = 0.06
VOLATILITY = 0.2
DISCOUNT = 0.02
DEFAULT_LOSS = 1.0 / 3.0


def local_dense(
    x_start, y_start, z_start, increments, default_step, term_weight, w_first, w_second, w_third
):
    steps = increments.shape[0]
    tstep = 1.0 / steps
    local_paths = increments.shape[1]
    scale = 1.0 / math.sqrt(local_paths * lax.axis_size("batch"))
    counter = jnp.arange(steps, dtype=jnp.int32)
    factors = (
        1.0
        + DISCOUNT * tstep
        - DEFAULT_LOSS * (counter[:, None] == default_step[None, :]).astype(jnp.float32)
    )
    states = jnp.broadcast_to(x_start[None, :], (local_paths, x_start.shape[0]))
    partials = [jnp.sum(increments[0] * z_start[None, :], axis=1)]
    states = states * (1.0 + DRIFT_RATE * tstep + VOLATILITY * increments[0])
    saved = []
    for index in range(1, steps):
        inputs_bf = lax.all_gather(states.astype(jnp.bfloat16), "dim", axis=1, tiled=True)
        tanh_first = jnp.tanh(
            jnp.dot(inputs_bf, w_first[index - 1], preferred_element_type=jnp.float32)
        )
        hidden_first = tanh_first.astype(jnp.bfloat16)
        part_second = jnp.dot(hidden_first, w_second[index - 1], preferred_element_type=jnp.float32)
        tanh_second = jnp.tanh(
            lax.psum_scatter(part_second, "dim", scatter_dimension=1, tiled=True)
        )
        hidden_second = lax.all_gather(tanh_second.astype(jnp.bfloat16), "dim", axis=1, tiled=True)
        control = jnp.dot(hidden_second, w_third[index - 1], preferred_element_type=jnp.float32)
        partials.append(jnp.sum(control * increments[index], axis=1))
        saved.append((inputs_bf, tanh_first, hidden_first, tanh_second, hidden_second))
        states = states * (1.0 + DRIFT_RATE * tstep + VOLATILITY * increments[index])
    target_part = jnp.sum(states * term_weight[None, :], axis=1) / math.sqrt(D)
    value = jnp.broadcast_to(y_start, (local_paths,))
    for index in range(steps):
        value = factors[index] * value + lax.psum(partials[index], "dim")
    target = lax.psum(target_part, "dim")
    error = value - target
    loss_local = scale * jnp.sum(error * error)
    adjoint = 2.0 * scale * error
    firsts, seconds, thirds = ([], [], [])
    for index in range(steps - 1, 0, -1):
        inputs_bf, tanh_first, hidden_first, tanh_second, hidden_second = saved[index - 1]
        d_control = (adjoint[:, None] * increments[index]).astype(jnp.bfloat16)
        grad_out = jnp.dot(hidden_second.T, d_control, preferred_element_type=jnp.float32)
        back_part = jnp.dot(d_control, w_third[index - 1].T, preferred_element_type=jnp.float32)
        back_share = lax.psum_scatter(back_part, "dim", scatter_dimension=1, tiled=True)
        d_share = (back_share * (1.0 - tanh_second * tanh_second)).astype(jnp.bfloat16)
        d_second = lax.all_gather(d_share, "dim", axis=1, tiled=True)
        grad_mid = jnp.dot(hidden_first.T, d_second, preferred_element_type=jnp.float32)
        back_first = jnp.dot(d_second, w_second[index - 1].T, preferred_element_type=jnp.float32)
        d_first = (back_first * (1.0 - tanh_first * tanh_first)).astype(jnp.bfloat16)
        grad_in = jnp.dot(inputs_bf.T, d_first, preferred_element_type=jnp.float32)
        firsts.append(grad_in)
        seconds.append(grad_mid)
        thirds.append(grad_out)
        adjoint = adjoint * factors[index]
    grad_z_part = jnp.sum(adjoint[:, None] * increments[0], axis=0)
    adjoint = adjoint * factors[0]
    grad_y_part = jnp.sum(adjoint)
    stack_first = jnp.stack(firsts[::-1])
    stack_second = jnp.stack(seconds[::-1])
    stack_third = jnp.stack(thirds[::-1])
    loss, grad_y, grad_z, stack_first, stack_second, stack_third = lax.psum(
        (loss_local, grad_y_part, grad_z_part, stack_first, stack_second, stack_third), "batch"
    )
    return (
        loss,
        grad_y,
        grad_z,
        stack_first.astype(jnp.bfloat16),
        stack_second.astype(jnp.bfloat16),
        stack_third.astype(jnp.bfloat16),
    )


MESH = pl.DeviceIdType.MESH
PAIR = 2


def remote(src, dst, sems, slot, target):
    return pltpu.make_async_remote_copy(
        src_ref=src,
        dst_ref=dst,
        send_sem=sems[0].at[slot],
        recv_sem=sems[1].at[slot],
        device_id=target,
        device_id_type=MESH,
    )


def greet(targets):
    barrier = pltpu.get_barrier_semaphore()
    for target in targets:
        pl.semaphore_signal(barrier, inc=1, device_id=target, device_id_type=MESH)
    pl.semaphore_wait(barrier, len(targets))


def flip(bit, turn):
    return 1 - bit if turn else bit


def here():
    row, me = lax.axis_index("batch"), lax.axis_index("dim")
    return row // PAIR, lax.rem(row, PAIR), me // PAIR, lax.rem(me, PAIR)


def device(level, side, chip, core):
    return {"batch": level * PAIR + side, "dim": chip * PAIR + core}


def hop(level, bit):
    low, high = lax.rem(level, PAIR), level // PAIR
    return flip(high, bit == 1) * PAIR + flip(low, bit == 0)


FLIPS = [(up, across, turn) for up in range(2) for across in range(2) for turn in range(2)]


def fetch_kernel(inc, state, third, first, second, inc_out, state_out, third_out, first_out, second_out, *sems):
    path_sems, core_sems, chip_sems, level_sems, pass_sems, last_sems = (
        (sems[2 * index], sems[2 * index + 1]) for index in range(6)
    )
    own, own_path = sems[12], sems[13]
    level, side, chip, core = here()
    me = chip * PAIR + core
    net = chip * PAIR + side
    across = (1 - chip) * PAIR + core
    partner = device(level, side, chip, 1 - core)
    beyond = device(level, side, 1 - chip, core)
    above = device(hop(level, 0), side, chip, core)
    half = lax.rem(level, PAIR)
    share, depth = inc.shape[2], second.shape[1]
    greet(
        [device(level, flip(side, up), flip(chip, ac), flip(core, turn)) for up, ac, turn in FLIPS[1:]]
        + [above]
    )

    def columns(source):
        return pl.ds(pl.multiple_of(source * share, share), share)

    def place(out, source, lines, part):
        if lines:
            cut = depth if part is None else depth // PAIR
            start = source * depth if part is None else source * depth + part * cut
            return out.at[pl.ds(pl.multiple_of(start, cut), cut), :]
        if part is None:
            return out.at[:, columns(source)]
        cut = out.shape[0] // PAIR
        return out.at[pl.ds(pl.multiple_of(part * cut, cut), cut), columns(source)]

    mats = [(third, third_out, False), (first, first_out, False), (second, second_out, True)]
    paths = [(inc, inc_out), (state, state_out)]

    def path_copy(index, up, ac):
        value, out = paths[index]
        to_chip, to_side = flip(chip, ac), flip(side, up)
        slot = ((index * 2 + up) * 2 + ac) * PAIR + core
        return remote(
            value.at[to_chip * PAIR + to_side], out.at[:, columns(me)], path_sems, slot,
            device(level, to_side, to_chip, side),
        )

    def path_arrival(index, up, ac, source):
        value, out = paths[index]
        slot = ((index * 2 + up) * 2 + ac) * PAIR + source
        return remote(value.at[0], out.at[:, columns(me)], path_sems, slot, partner)

    def path_own(index):
        value, out = paths[index]
        return pltpu.make_async_copy(value.at[net], out.at[:, columns(me)], own_path.at[index])

    aligned = core == side
    chip_copies, waits = [], []
    for index, (value, out, lines) in enumerate(mats):
        cut = value.shape[1] // PAIR
        copy = remote(
            value.at[(1 - chip) * PAIR + side, pl.ds(pl.multiple_of(half * cut, cut), cut), :],
            place(out, me, lines, half), chip_sems, index, beyond,
        )
        copy.start()
        chip_copies.append(copy)

    for index in range(2):
        for up, ac in ((0, 1), (1, 1), (1, 0)):
            path_copy(index, up, ac).start()

    @pl.when(aligned)
    def _():
        for index in range(2):
            path_own(index).start()

    @pl.when(jnp.logical_not(aligned))
    def _():
        for index in range(2):
            path_copy(index, 0, 0).start()

    for index, (value, out, lines) in enumerate(mats):
        copy = remote(value.at[net], place(out, me, lines, None), core_sems, index, partner)
        copy.start()
        waits.append(copy)
        copy = pltpu.make_async_copy(value.at[net], place(out, me, lines, None), own.at[index])
        copy.start()
        waits.append(copy)
    level_copies = []
    for index, (value, out, lines) in enumerate(mats):
        chip_copies[index].wait_recv()
        spot = place(out, across, lines, half)
        copy = remote(spot, spot, level_sems, index, above)
        copy.start()
        level_copies.append(copy)
        copy = remote(spot, spot, pass_sems, index, partner)
        copy.start()
        waits.append(copy)
    for index, (value, out, lines) in enumerate(mats):
        level_copies[index].wait_recv()
        spot = place(out, across, lines, 1 - half)
        copy = remote(spot, spot, last_sems, index, partner)
        copy.start()
        waits.append(copy)
    for copy in chip_copies + level_copies:
        copy.wait_send()
    for index in range(2):
        for up, ac in ((0, 1), (1, 1), (1, 0)):
            path_copy(index, up, ac).wait_send()

    @pl.when(aligned)
    def _():
        for index in range(2):
            path_own(index).wait()
            path_arrival(index, 0, 0, 1 - core).wait_recv()
            for source in range(PAIR):
                path_arrival(index, 0, 1, source).wait_recv()

    @pl.when(jnp.logical_not(aligned))
    def _():
        for index in range(2):
            path_copy(index, 0, 0).wait_send()
            for ac in range(2):
                for source in range(PAIR):
                    path_arrival(index, 1, ac, source).wait_recv()

    for copy in waits:
        copy.wait()


def fetch(inc, state, third, first, second):
    nets = third.shape[0]
    paths, width, hidden = inc.shape[1], first.shape[1], second.shape[2]
    any_spec = pl.BlockSpec(memory_space=pl.ANY)
    counts = [4 * nets, 3, 3, 3, 3, 3]
    return pl.pallas_call(
        fetch_kernel,
        out_shape=(
            jax.ShapeDtypeStruct((paths, width), inc.dtype),
            jax.ShapeDtypeStruct((paths, width), state.dtype),
            jax.ShapeDtypeStruct((hidden, width), third.dtype),
            jax.ShapeDtypeStruct((width, hidden), first.dtype),
            jax.ShapeDtypeStruct((hidden, hidden), second.dtype),
        ),
        in_specs=[pl.BlockSpec(memory_space=pltpu.VMEM)] * 5,
        out_specs=(any_spec,) * 5,
        scratch_shapes=[pltpu.SemaphoreType.DMA((count,)) for count in counts for _ in range(2)]
        + [pltpu.SemaphoreType.DMA((3,)), pltpu.SemaphoreType.DMA((2,))],
        compiler_params=pltpu.CompilerParams(
            collective_id=0, has_side_effects=True, vmem_limit_bytes=16 * 1024 * 1024
        ),
        name="fetch",
    )(inc, state, third, first, second)


def share_kernel(block, out, gathered, send, recv):
    level, side, chip, core = here()
    targets = [device(level, flip(side, up), flip(chip, ac), flip(core, turn)) for up, ac, turn in FLIPS[1:]]
    greet(targets)
    copies = []
    for index, target in enumerate(targets):
        copy = remote(block, gathered.at[side, chip * PAIR + core], (send, recv), index, target)
        copy.start()
        copies.append(copy)
    gathered[side, chip * PAIR + core] = block[...]
    for copy in copies:
        copy.wait()
    out[...] = gathered[...]


def share_level(block, nets):
    shape = (PAIR, nets) + block.shape
    vmem = pl.BlockSpec(memory_space=pltpu.VMEM)
    return pl.pallas_call(
        share_kernel,
        out_shape=jax.ShapeDtypeStruct(shape, block.dtype),
        in_specs=[vmem],
        out_specs=vmem,
        scratch_shapes=[pltpu.VMEM(shape, block.dtype)]
        + [pltpu.SemaphoreType.DMA((len(FLIPS) - 1,))] * 2,
        compiler_params=pltpu.CompilerParams(collective_id=2, has_side_effects=True),
        name="share_level",
    )(block)


def reduce_kernel(rows, nets, *refs):
    lefts, rights, refs = refs[0:3], refs[3:6], refs[6:]
    small, outs, small_out, grads = refs[0], refs[1:4], refs[4], refs[5:8]
    zero, one, two = refs[8:11], refs[11:14], refs[14:17]
    sent_one, sent_two, held = refs[17:20], refs[20:23], refs[23:26]
    gathered = refs[26]
    zero_sems, one_sems, two_sems, back_two, back_one, out_sems, small_sems = (
        (refs[27 + 2 * index], refs[28 + 2 * index]) for index in range(7)
    )
    own = refs[41]
    f32, bf16 = jnp.float32, jnp.bfloat16
    level, side, chip, core = here()
    row = level * PAIR + side
    net = chip * PAIR + side
    low, high = lax.rem(level, PAIR), level // PAIR
    slot_mine = low * PAIR + high
    partner = device(level, side, chip, 1 - core)
    first, second = (device(hop(level, bit), side, chip, core) for bit in range(2))
    mats = range(3)
    cuts = [grad.shape[1] // rows for grad in grads]
    chunks = [(mat, turn) for turn in (1, 0) for mat in (2, 1, 0)]
    others = [(up, ac, turn) for up, ac, turn in FLIPS if (up, ac, turn) != (0, 0, 0)]
    greet(
        [{"batch": lax.rem(row + jump, rows)} for jump in range(1, rows)]
        + [device(level, flip(side, up), flip(chip, ac), flip(core, turn)) for up, ac, turn in others if ac or turn]
    )

    def shards(turn):
        return pl.ds(flip(chip, turn) * PAIR, PAIR)

    def span(mat, start, count):
        return pl.ds(pl.multiple_of(start * cuts[mat], cuts[mat]), count * cuts[mat])

    copies = {}

    def core_step(index):
        mat, turn = chunks[index]
        for part in range(PAIR):
            shard = flip(chip, turn) * PAIR + part
            depth, width = grads[mat].shape[1:]
            left, right = lefts[mat][...], rights[mat]
            if width == right.shape[1]:
                left = lefts[mat][:, pl.ds(pl.multiple_of(shard * depth, depth), depth)]
                right = right[...]
            else:
                right = right[:, pl.ds(pl.multiple_of(shard * width, width), width)]
            grads[mat][shard] = lax.dot_general(
                left, right, (((0,), (0,)), ((), ())), preferred_element_type=f32
            ).astype(bf16)
        copy = remote(
            grads[mat].at[shards(turn), span(mat, (1 - core) * 4, 4), :],
            zero[mat].at[shards(turn)], zero_sems, index, partner,
        )
        copy.start()
        copies["zero", index] = copy

    def low_step(index):
        mat, turn = chunks[index]
        copies["zero", index].wait_recv()
        start = (1 - low) * 2
        value = grads[mat][shards(turn), span(mat, core * 4 + start, 2), :].astype(f32)
        value = value + zero[mat][shards(turn), span(mat, start, 2), :].astype(f32)
        sent_one[mat][shards(turn)] = value.astype(bf16)
        copy = remote(
            sent_one[mat].at[shards(turn)], one[mat].at[shards(turn)], one_sems, index, first
        )
        copy.start()
        copies["one", index] = copy

    def partial(mat, turn, end):
        value = grads[mat][shards(turn), span(mat, core * 4 + low * 2 + end, 1), :].astype(f32)
        value = value + zero[mat][shards(turn), span(mat, low * 2 + end, 1), :].astype(f32)
        return value + one[mat][shards(turn), span(mat, end, 1), :].astype(f32)

    def high_step(index):
        mat, turn = chunks[index]
        copies["one", index].wait_recv()
        sent_two[mat][shards(turn)] = partial(mat, turn, 1 - high).astype(bf16)
        copy = remote(
            sent_two[mat].at[shards(turn)], two[mat].at[shards(turn)], two_sems, index, second
        )
        copy.start()
        copies["two", index] = copy

    def spread(index, event, slot, count):
        mat, turn = chunks[index]
        lines = span(mat, core * 4 + slot, count)
        for up in range(2):
            for swapped in range(2):
                shard = flip(chip, turn) * PAIR + flip(core, swapped)
                src = held[mat].at[shard, span(mat, slot, count), :]
                dst = outs[mat].at[net, lines, :]
                if up or turn or swapped:
                    number = ((index * 3 + event) * 2 + up) * 2 + swapped
                    copy = remote(
                        src, dst, out_sems, number,
                        device(level, flip(side, up), flip(chip, turn), flip(core, swapped)),
                    )
                else:
                    copy = pltpu.make_async_copy(src, dst, own.at[index * 3 + event])
                copy.start()
                copies["out", index, event, up, swapped] = copy

    def final_step(index):
        mat, turn = chunks[index]
        copies["two", index].wait_recv()
        value = partial(mat, turn, high) + two[mat][shards(turn)].astype(f32)
        held[mat][shards(turn), span(mat, slot_mine, 1), :] = value.astype(bf16)
        spot = held[mat].at[shards(turn), span(mat, slot_mine, 1), :]
        for name, sems, target in (("back_two", back_two, second), ("back_one", back_one, first)):
            copy = remote(spot, spot, sems, index * 2 if name == "back_one" else index, target)
            copy.start()
            copies[name, index] = copy
        spread(index, 0, slot_mine, 1)

    def gather_step(index):
        mat, turn = chunks[index]
        copies["back_two", index].wait_recv()
        slot = low * PAIR + 1 - high
        spot = held[mat].at[shards(turn), span(mat, slot, 1), :]
        copy = remote(spot, spot, back_one, index * 2 + 1, first)
        copy.start()
        copies["back_far", index] = copy
        spread(index, 1, slot, 1)

    def last_step(index):
        copies["back_one", index].wait_recv()
        copies["back_far", index].wait_recv()
        spread(index, 2, (1 - low) * PAIR, PAIR)

    small_copies = []
    for jump in range(1, rows):
        copy = remote(small, gathered.at[row], small_sems, jump - 1, {"batch": lax.rem(row + jump, rows)})
        copy.start()
        small_copies.append(copy)
    gathered[row] = small[...]
    stages = (
        (0, core_step),
        (1, low_step),
        (3, high_step),
        (5, final_step),
        (6, gather_step),
        (8, last_step),
    )
    for time in range(len(chunks) + stages[-1][0]):
        for lag, stage in reversed(stages):
            if 0 <= time - lag < len(chunks):
                stage(time - lag)
    for copy in small_copies:
        copy.wait()
    summed = gathered[0]
    for index in range(1, rows):
        summed = summed + gathered[index]
    small_out[...] = summed
    for name, copy in copies.items():
        if name[0] == "out":
            copy.wait()
        else:
            copy.wait_send()


def reduce_grads(lefts, rights, small, shapes, rows):
    nets = shapes[0][0]
    bf16 = jnp.bfloat16
    any_spec = pl.BlockSpec(memory_space=pl.ANY)
    vmem = pl.BlockSpec(memory_space=pltpu.VMEM)
    chunks = 3 * PAIR

    def pieces(count):
        return [
            pltpu.VMEM((nets, count * (shape[1] // rows), shape[2]), bf16) for shape in shapes
        ]

    def dma(count):
        return [pltpu.SemaphoreType.DMA((count,))] * 2

    return pl.pallas_call(
        functools.partial(reduce_kernel, rows, nets),
        out_shape=tuple(jax.ShapeDtypeStruct(shape, bf16) for shape in shapes)
        + (jax.ShapeDtypeStruct(small.shape, small.dtype),),
        in_specs=[vmem] * 7,
        out_specs=(any_spec,) * 3 + (vmem,),
        scratch_shapes=pieces(rows)
        + pieces(4)
        + pieces(2)
        + pieces(1)
        + pieces(2)
        + pieces(1)
        + pieces(4)
        + [pltpu.VMEM((rows,) + small.shape, small.dtype)]
        + dma(chunks)
        + dma(chunks)
        + dma(chunks)
        + dma(chunks)
        + dma(chunks * 2)
        + dma(chunks * 12)
        + dma(rows - 1)
        + [pltpu.SemaphoreType.DMA((chunks * 3,))],
        compiler_params=pltpu.CompilerParams(
            collective_id=1, has_side_effects=True, vmem_limit_bytes=36 * 1024 * 1024
        ),
        name="reduce_grads",
    )(*lefts, *rights, small)


def local_nets(
    x_start, y_start, z_start, increments, default_step, term_weight, w_first, w_second, w_third
):
    f32, bf16 = jnp.float32, jnp.bfloat16
    steps, paths, share = increments.shape
    nets = steps - 1
    width = w_first.shape[1]
    hidden = w_second.shape[2]
    rows = lax.axis_size("batch")
    tstep = 1.0 / steps
    scale = 1.0 / math.sqrt(paths * rows)
    me = lax.axis_index("dim")
    counter = jnp.arange(steps, dtype=jnp.int32)
    states = jnp.broadcast_to(x_start[None, :], (paths, share))
    dot_start = jnp.sum(increments[0] * z_start[None, :], axis=1)
    sent = []
    for index in range(steps):
        if index > 0:
            sent.append(states.astype(bf16))
        states = states * (1.0 + DRIFT_RATE * tstep + VOLATILITY * increments[index])
    target_part = jnp.sum(states * term_weight[None, :], axis=1) / math.sqrt(share * lax.axis_size("dim"))

    inc, inputs, third, first, second = fetch(
        increments[1:], jnp.stack(sent), w_third, w_first, w_second
    )
    high = inc.astype(bf16)
    low = (inc - high.astype(f32)).astype(bf16)
    back = jnp.dot(high, third.T, preferred_element_type=f32) + jnp.dot(
        low, third.T, preferred_element_type=f32
    )
    tanh_first = jnp.tanh(jnp.dot(inputs, first, preferred_element_type=f32))
    hidden_first = tanh_first.astype(bf16)
    tanh_second = jnp.tanh(jnp.dot(hidden_first, second, preferred_element_type=f32))
    hidden_second = tanh_second.astype(bf16)
    dot_mine = jnp.sum(hidden_second.astype(f32) * back, axis=1)
    slope_second = back * (1.0 - tanh_second * tanh_second)
    slope_first = jnp.dot(slope_second.astype(bf16), second.T, preferred_element_type=f32) * (
        1.0 - tanh_first * tanh_first
    )
    block = jnp.zeros((8, paths), f32)
    block = block.at[0].set(dot_mine).at[1].set(dot_start).at[2].set(target_part)
    block = block.at[3].set(default_step.astype(f32))
    shared = share_level(block, nets)
    side, core = lax.rem(lax.axis_index("batch"), PAIR), lax.rem(me, PAIR)
    net = me // PAIR * PAIR + side
    falls = shared[:, 0, 3]
    factors = (
        1.0
        + DISCOUNT * tstep
        - DEFAULT_LOSS * (counter[:, None, None].astype(f32) == falls[None]).astype(f32)
    )
    value = factors[0] * y_start + jnp.sum(shared[:, :, 1], axis=1)
    for index in range(1, steps):
        chip, low = divmod(index - 1, PAIR)
        dots = shared[low, chip * PAIR : (chip + 1) * PAIR, 0]
        value = factors[index] * value + dots
    error = value - jnp.sum(shared[:, :, 2], axis=1)
    adjoint = 2.0 * scale * error
    adjoints = []
    for index in range(steps - 1, 0, -1):
        adjoints.append(adjoint)
        adjoint = adjoint * factors[index]
    start = lax.dynamic_index_in_dim(adjoint, side, keepdims=False)
    grad_z_part = jnp.sum(start[:, None] * increments[0], axis=0)
    grad_y_part = jnp.sum(start * lax.dynamic_index_in_dim(factors[0], side, keepdims=False))
    fault = lax.dynamic_index_in_dim(error, side, keepdims=False)
    loss_local = scale * jnp.sum(fault * fault)
    mine = lax.dynamic_index_in_dim(jnp.stack(adjoints[::-1]), net, keepdims=False)
    mine = lax.dynamic_index_in_dim(mine, core, keepdims=False)[:, None]

    small = jnp.zeros((8, share), f32)
    small = small.at[0].set(grad_z_part).at[1].set(loss_local).at[2].set(grad_y_part)
    rights = tuple((mine * value).astype(bf16) for value in (slope_first, slope_second, inc))
    grad_first, grad_second, grad_third, small = reduce_grads(
        (inputs, hidden_first, hidden_second),
        rights,
        small,
        (w_first.shape, w_second.shape, w_third.shape),
        rows,
    )
    return small[1, 0], small[2, 0], small[0], grad_first, grad_second, grad_third


def pick(mesh):
    def run(*args):
        nets = args[6].shape[0]
        rows = mesh.shape["batch"]
        fits = mesh.shape["dim"] == nets == PAIR * PAIR and rows == PAIR * PAIR * PAIR
        return (local_nets if fits else local_dense)(*args)

    return run


def solution(mesh):
    placed = (
        P("dim"),
        P(),
        P("dim"),
        P(None, "batch", "dim"),
        P("batch"),
        P("dim"),
        P(None, None, "dim"),
        P(None, "dim", None),
        P(None, None, "dim"),
    )
    return jax.shard_map(
        pick(mesh),
        mesh=mesh,
        in_specs=placed,
        out_specs=(
            P(),
            P(),
            P("dim"),
            P(None, None, "dim"),
            P(None, "dim", None),
            P(None, None, "dim"),
        ),
        check_vma=False,
    )
```
